32 devices in a mesh: energy: 8 (over y, x, core), kpt: 4 (over z).
Axes of the slice: x: 2, y: 2, z: 4, core: 2. Of those that a mesh axis runs over, the one named last changes fastest.
Arguments:
- density: bfloat16 [32, 4, 64, 3072], P('energy', 'kpt'), may hold values from -6 to 6
- quad_weights: float32 [32, 4], P('energy', 'kpt'), may hold values from 0.044194173 to 0.17677669
- orbital_cells: int32 [64, 3072], replicated, may hold values from 0 to 131071
- fixed_charge: float32 [512, 64, 256], P('energy', 'kpt'), may hold values from -16 to 16
- gate_mask: int32 [512, 64, 256], P('energy', 'kpt'), may hold values 0 or 1
- gate_voltage: float32 [512], P('energy'), may hold values from -1 to 1
Outputs:
- potential: float32 [512, 64, 256], P('energy', 'kpt')
- band_shift: float32 [32, 4, 64], P('energy', 'kpt')
The draws below stay inside these ranges and needn't reach their ends.
Inputs may be any that keep to these rules, and one draw needn't show every extreme that they name: `orbital_cells`: each entry is s * 64 * 256 + y * 256 + z, a cell of one of the layer's 8 planes.
All inputs are finite; a program needn't handle non-finite values. No bound on the sum of `gate_mask` on one device may be relied on, other than what follows from the above.
Results may differ from the reference program's by a relative error of at most 0.0003.
Values sent between devices are 32-bit elements; how exact they have to be, the bound alone decides.
A program may use at most 64 MiB of HBM per device.

```python
import math
import jax
import jax.numpy as jnp
from jax import lax

ORBITALS = 3072
SUB = 8
CY = 16
NZ = 256
ITERS = 2
ENERGIES = 32
KPOINTS = 4
LAYERS = 64
NY = 64
CX = 64
GX = 512


def draw_fixed_charge(key, part):
    blocks_x = GX // CX
    blocks_y = NY // CY
    block_count = blocks_x * blocks_y
    ranking = jax.random.permutation(jax.random.fold_in(key, 12), block_count)
    chosen = (ranking < block_count // 2).astype(jnp.float32)
    phases = jax.random.uniform(jax.random.fold_in(key, 14), (3,), jnp.float32, 0.0, 2.0 * math.pi)
    white_noise = jnp.clip(jax.random.normal(jax.random.fold_in(key, 11), (GX, NY, NZ), jnp.float32), -6.0, 6.0)
    levels = jax.random.uniform(jax.random.fold_in(key, 13), (block_count,), jnp.float32, 1.5, 3.0) * chosen
    block_level = jnp.repeat(jnp.repeat(levels.reshape(blocks_x, blocks_y), CX, axis=0), CY, axis=1)
    plane_pos = (jnp.arange(GX, dtype=jnp.float32) + 0.5) / GX
    column_pos = (jnp.arange(NY, dtype=jnp.float32) + 0.5) / NY
    depth_pos = (jnp.arange(NZ, dtype=jnp.float32) + 0.5) / NZ
    plane_wave = jnp.sin(2.0 * math.pi * plane_pos + phases[0])
    column_wave = jnp.sin(2.0 * math.pi * column_pos + phases[1])
    depth_wave = jnp.sin(2.0 * math.pi * depth_pos + phases[2])
    smooth_field = 1.0 + 0.5 * plane_wave[:, None, None] * depth_wave[None, None, :] + 0.4 * column_wave[None, :, None]
    return (white_noise + block_level[:, :, None] * smooth_field).astype(jnp.float32)


def with_ends(values, stream_key, smallest, largest):
    longest = values.shape.index(max(values.shape))
    spots = []
    for shift in (0, 1):
        where = [jax.random.randint(jax.random.fold_in(stream_key, axis), (), 0, length) for axis, length in enumerate(values.shape)]
        where[longest] = (where[longest] + shift) % values.shape[longest]
        spots.append(tuple(where))
    return values.at[spots[0]].set(smallest).at[spots[1]].set(largest)


def strengthened(entries, rng, source, target, shards_of, factor):
    owner, partner = [(jnp.arange(entries.shape[axis_at]) // (entries.shape[axis_at] // shards_of)).reshape([-1 if axis == axis_at else 1 for axis in range(entries.ndim)]) for axis_at in (source, target)]
    chosen = jax.random.permutation(rng, shards_of)[partner]
    strong = (owner == chosen) | (owner == (partner + shards_of // 2) % shards_of)
    return jnp.where(strong, factor * entries, entries)


def block_levels(rng, dims, pieces, smallest, top_value):
    def one(position, parts):
        heights = jax.random.uniform(jax.random.fold_in(jax.random.fold_in(rng, 6), position), (parts,), jnp.float32, smallest / len(pieces), top_value / len(pieces))
        return jnp.repeat(jnp.exp(heights), dims[position] // parts).reshape((-1,) + (1,) * (len(dims) - position - 1))

    gain = one(*pieces[0])
    for cut in pieces[1:]:
        gain = gain * one(*cut)
    return gain


def gaussian_with(own_key, shape, scale, most, shards, heavy, kind=jnp.bfloat16):
    values = scale * jax.random.normal(own_key, shape, jnp.float32)
    if shards:
        values = values * block_levels(own_key, shape, shards, -0.22, 0.18)
    return jnp.clip(strengthened(values, jax.random.fold_in(own_key, 3), *heavy), -most, most).astype(kind)


def setup_inputs(seed: int = 0) -> dict:
    seeds = jax.random.split(jax.random.key(seed), 7)
    return {
        "density": gaussian_with(seeds[0], (ENERGIES, KPOINTS, LAYERS, ORBITALS), 1.0, 6.0, ((0, 8), (1, 4)), (0, 2, 8, 2.0)),
        "quad_weights": jnp.clip(jnp.exp(math.log(0.17677669) - 1.3862944 * jax.random.uniform(seeds[1], (ENERGIES, KPOINTS), jnp.float32) ** block_levels(seeds[1], (ENERGIES, KPOINTS), ((0, 8), (1, 4)), -0.2, 0.2)), 0.044194173, 0.17677669),
        "orbital_cells": with_ends(jax.random.randint(seeds[2], (LAYERS, ORBITALS), 0, SUB * NY * NZ), jax.random.fold_in(seeds[2], 1), 0, (SUB * NY * NZ) - 1).astype(jnp.int32),
        "fixed_charge": draw_fixed_charge(jax.random.fold_in(seeds[6], 71), 0),
        "gate_mask": with_ends((jax.random.randint(seeds[4], (GX, NY, NZ), 0, 4) < 1).astype(jnp.int32), jax.random.fold_in(seeds[4], 1), 0, 1),
        "gate_voltage": jnp.clip(jax.random.uniform(seeds[5], (GX,), jnp.float32, -1.0, 1.0) * block_levels(seeds[5], (GX,), ((0, 8),), -0.4, 0.0), -1.0, 1.0),
    }


PENALTY = 4.0


def operate(values_field, diagonal):
    padded = jnp.pad(values_field, 1)
    beside = padded[2:, 1:-1, 1:-1] + padded[:-2, 1:-1, 1:-1]
    beside = beside + padded[1:-1, 2:, 1:-1] + padded[1:-1, :-2, 1:-1]
    beside = beside + padded[1:-1, 1:-1, 2:] + padded[1:-1, 1:-1, :-2]
    return diagonal * values_field - beside


def reference(density, quad_weights, orbital_cells, fixed_charge, gate_mask, gate_voltage):
    occupancy = jnp.einsum("ek,eklo->lo", quad_weights.astype(jnp.float32), density.astype(jnp.float32), precision=lax.Precision.HIGHEST)
    section = SUB * NY * NZ
    layer_base = (jnp.arange(LAYERS, dtype=jnp.int32) * section)[:, None]
    flat_cell = (orbital_cells + layer_base).reshape(-1)
    charge = jax.ops.segment_sum(occupancy.reshape(-1), flat_cell, num_segments=LAYERS * section).reshape(GX, NY, NZ)
    gated = gate_mask.astype(jnp.float32)
    diagonal = 6.0 + PENALTY * gated
    right_side = fixed_charge - charge + PENALTY * gated * gate_voltage[:, None, None]
    potential = jnp.zeros_like(right_side)
    residual = right_side
    direction = right_side
    norm_now = jnp.sum(residual * residual)
    for sweep_index in range(ITERS):
        image = operate(direction, diagonal)
        alpha = norm_now / jnp.sum(direction * image)
        potential = potential + alpha * direction
        residual = residual - alpha * image
        norm_next = jnp.sum(residual * residual)
        direction = residual + (norm_next / norm_now) * direction
        norm_now = norm_next
    orbital_potential = jnp.take_along_axis(potential.reshape(LAYERS, section), orbital_cells, axis=1)
    band_shift = jnp.einsum("eklo,lo->ekl", density.astype(jnp.float32), orbital_potential, precision=lax.Precision.HIGHEST) * (ORBITALS ** -0.5)
    return potential, band_shift
```

```python
import functools

import jax
import jax.numpy as jnp
from jax import lax
from jax.experimental import pallas as pl
from jax.experimental.pallas import tpu as pltpu
from jax.sharding import PartitionSpec as P

PENALTY = 4.0
MESH = pl.DeviceIdType.MESH
F32 = jnp.float32
BF16 = jnp.bfloat16
VMEM = pl.BlockSpec(memory_space=pltpu.VMEM)
SMEM = pl.BlockSpec(memory_space=pltpu.SMEM)
DMA = pltpu.SemaphoreType.DMA


def place():
    return lax.axis_index("energy"), lax.axis_index("kpt")


def enter(ne, nk):
    e, k = place()
    barrier = pltpu.get_barrier_semaphore()
    for step in range(1, ne):
        pl.semaphore_signal(
            barrier, inc=1, device_id=(lax.rem(e + step, ne), k), device_id_type=MESH
        )
    for step in range(1, nk):
        pl.semaphore_signal(
            barrier, inc=1, device_id=(e, lax.rem(k + step, nk)), device_id_type=MESH
        )
    pl.semaphore_wait(barrier, ne + nk - 2)


def send(src, dst, send_sem, recv_sem, target):
    copy = pltpu.make_async_remote_copy(
        src_ref=src,
        dst_ref=dst,
        send_sem=send_sem,
        recv_sem=recv_sem,
        device_id=target,
        device_id_type=MESH,
    )
    copy.start()
    return copy


def reduce_kernel(ne, nk, density, weights, out, mine, land, part, kland, es, er, ks, kr):
    e, k = place()
    points = density.shape[0]

    def slab_sum(t):
        total = weights[0, 0] * density[0, t].astype(F32)
        for q in range(1, points):
            total = total + weights[q, 0] * density[q, t].astype(F32)
        return total

    enter(ne, nk)
    copies = []
    for step in range(1, ne):
        t = lax.rem(e + step, ne)
        mine[step] = slab_sum(t)
        copies.append(send(mine.at[step], land.at[step], es.at[step], er.at[step], (t, k)))
    total = slab_sum(e)
    for step in range(1, ne):
        copies[step - 1].wait_recv()
        total = total + land[step]
    part[...] = total
    hops = []
    for step in range(1, nk):
        t = lax.rem(k + step, nk)
        hops.append(send(part, kland.at[step], ks.at[step], kr.at[step], (e, t)))
    for step in range(1, nk):
        hops[step - 1].wait_recv()
        total = total + kland[step]
    out[...] = total
    for copy in copies + hops:
        copy.wait_send()


def halves(values):
    high = values.astype(BF16)
    return high, (values - high.astype(F32)).astype(BF16)


def one_hot(count, index):
    iota = lax.broadcasted_iota(jnp.int32, (count, index.shape[1]), 0)
    return iota == index


def deposit_kernel(slab, sub, row_of, depth_of, occupancy, base, out):
    wy, nz = out.shape[1:]
    rows = sub * wy

    def layer(l, carry):
        hit = one_hot(rows, row_of[pl.ds(l, 1), :])
        value = occupancy[pl.ds(l, 1), :]
        high = value.astype(BF16).astype(F32)
        left = jnp.concatenate(
            [jnp.where(hit, high, 0.0).astype(BF16), jnp.where(hit, value - high, 0.0).astype(BF16)],
            axis=0,
        )
        right = jnp.where(one_hot(nz, depth_of[pl.ds(l, 1), :]), 1.0, 0.0).astype(BF16)
        both = lax.dot_general(left, right, (((1,), (1,)), ((), ())), preferred_element_type=F32)
        charge = (both[:rows] + both[rows:]).reshape(sub, wy, nz)
        out[pl.ds(l * sub, sub)] = base[pl.ds(l * sub, sub)] - charge
        return carry

    lax.fori_loop(0, slab, layer, 0)


def krylov_kernel(
    ne, nk, chunk, right_side, gate, image, stats, field, edge, halo, sums, eland, ksum, kland,
    xs, xr, ys, yr, es, er, ks, kr
):
    e, k = place()
    planes, wy, nz = right_side.shape
    enter(ne, nk)
    for v in range(2):
        @pl.when(e == 0)
        def _():
            field[v, 0] = jnp.zeros((wy, nz), F32)

        @pl.when(e == ne - 1)
        def _():
            field[v, planes + 1] = jnp.zeros((wy, nz), F32)

        @pl.when(k == 0)
        def _():
            halo[v, 0] = jnp.zeros((planes, nz), F32)

        @pl.when(k == nk - 1)
        def _():
            halo[v, 1] = jnp.zeros((planes, nz), F32)

    def fill(i, carry):
        b = i * chunk
        block = right_side[pl.ds(b, chunk)]
        field[0, pl.ds(b + 1, chunk)] = block
        edge[0, 0, pl.ds(b, chunk), :] = block[:, 0, :]
        edge[0, 1, pl.ds(b, chunk), :] = block[:, wy - 1, :]
        return carry

    lax.fori_loop(0, planes // chunk, fill, 0)

    def copies(v):
        def make(src, dst, ss, rs, target):
            return pltpu.make_async_remote_copy(
                src_ref=src, dst_ref=dst, send_sem=ss, recv_sem=rs,
                device_id=target, device_id_type=MESH,
            )

        up = make(field.at[v, planes], field.at[v, 0], xs.at[v, 0], xr.at[v, 0], (lax.rem(e + 1, ne), k))
        down = make(field.at[v, 1], field.at[v, planes + 1], xs.at[v, 1], xr.at[v, 1], (lax.rem(e + ne - 1, ne), k))
        right = make(edge.at[v, 1], halo.at[v, 0], ys.at[v, 0], yr.at[v, 0], (e, lax.rem(k + 1, nk)))
        left = make(edge.at[v, 0], halo.at[v, 1], ys.at[v, 1], yr.at[v, 1], (e, lax.rem(k + nk - 1, nk)))
        return ((up, e < ne - 1, e > 0), (down, e > 0, e < ne - 1), (right, k < nk - 1, k > 0), (left, k > 0, k < nk - 1))

    def start(v):
        for copy, sends, _ in copies(v):
            pl.when(sends)(copy.start)

    def arrive(v):
        for copy, _, receives in copies(v):
            pl.when(receives)(copy.wait_recv)

    row = lax.broadcasted_iota(jnp.int32, (chunk, wy, nz), 1)
    lane = lax.broadcasted_iota(jnp.int32, (chunk, wy, nz), 2)

    def applied(v, b):
        here = field[v, pl.ds(b + 1, chunk)]
        near = field[v, pl.ds(b, chunk)] + field[v, pl.ds(b + 2, chunk)]
        low = halo[v, 0, pl.ds(b, chunk), :].reshape(chunk, 1, nz)
        high = halo[v, 1, pl.ds(b, chunk), :].reshape(chunk, 1, nz)
        near = near + jnp.where(row == 0, low, pltpu.roll(here, 1, 1))
        near = near + jnp.where(row == wy - 1, high, pltpu.roll(here, wy - 1, 1))
        near = near + jnp.where(lane == 0, 0.0, pltpu.roll(here, 1, 2))
        near = near + jnp.where(lane == nz - 1, 0.0, pltpu.roll(here, nz - 1, 2))
        diagonal = 6.0 + PENALTY * gate[pl.ds(b, chunk)].astype(F32)
        return here, diagonal * here - near

    start(0)
    arrive(0)
    zero = jnp.zeros((wy, nz), F32)

    def first(i, carry):
        rr, rw, ww = carry
        b = i * chunk
        here, w = applied(0, b)
        field[1, pl.ds(b + 1, chunk)] = w
        image[pl.ds(b, chunk)] = w
        edge[1, 0, pl.ds(b, chunk), :] = w[:, 0, :]
        edge[1, 1, pl.ds(b, chunk), :] = w[:, wy - 1, :]
        return rr + jnp.sum(here * here, axis=0), rw + jnp.sum(here * w, axis=0), ww + jnp.sum(w * w, axis=0)

    rr, rw, ww = lax.fori_loop(0, planes // chunk, first, (zero, zero, zero))
    start(1)
    arrive(1)

    def second(i, wv):
        here, image_two = applied(1, i * chunk)
        return wv + jnp.sum(here * image_two, axis=0)

    wv = lax.fori_loop(0, planes // chunk, second, zero)
    sums[...] = jnp.zeros(sums.shape, F32)
    for i, acc in enumerate((rr, rw, ww, wv)):
        line = jnp.sum(acc, axis=0, keepdims=True)
        width = sums.shape[1]
        folded = line[:, :width]
        for at in range(width, nz, width):
            folded = folded + line[:, at : at + width]
        sums[i : i + 1, :] = folded
    outs = []
    for step in range(1, ne):
        outs.append(send(sums, eland.at[step], es.at[step], er.at[step], (lax.rem(e + step, ne), k)))
    total = sums[...]
    for step in range(1, ne):
        outs[step - 1].wait_recv()
        total = total + eland[step]
    ksum[...] = total
    for step in range(1, nk):
        outs.append(send(ksum, kland.at[step], ks.at[step], kr.at[step], (e, lax.rem(k + step, nk))))
    for step in range(1, nk):
        outs[ne - 2 + step].wait_recv()
        total = total + kland[step]
    stats[...] = total
    for copy in outs:
        copy.wait_send()
    for v in range(2):
        for copy, sends, _ in copies(v):
            pl.when(sends)(copy.wait_send)


def gather_kernel(slab, sub, nk, row_of, depth_of, right_side, image, stats, potential, local):
    wy, nz = right_side.shape[1:]
    rows = sub * wy
    sums = jnp.sum(stats[...], axis=1, keepdims=True)
    rr, rw, ww, wv = (sums[i : i + 1, :] for i in range(4))
    alpha = rr / rw
    norm_next = rr - 2.0 * alpha * rw + alpha * alpha * ww
    product = rw - 2.0 * alpha * ww + alpha * alpha * wv
    ratio = norm_next / rr
    alpha_two = norm_next / (product - ratio * norm_next / alpha)
    by_right = (alpha + alpha_two * (1.0 + ratio)).reshape(1, 1, 1)
    by_image = (alpha_two * alpha).reshape(1, 1, 1)
    cols = local.shape[2]

    def layer(l, carry):
        at = pl.ds(l * sub, sub)
        value = by_right * right_side[at] - by_image * image[at]
        potential[at] = value
        high, low = halves(value.reshape(rows, nz))
        left = jnp.concatenate([high, low], axis=0)
        right = jnp.where(one_hot(nz, depth_of[pl.ds(l, 1), :]), 1.0, 0.0).astype(BF16)
        both = jnp.dot(left, right, preferred_element_type=F32)
        hit = one_hot(rows, row_of[pl.ds(l, 1), :])
        picked = jnp.sum(jnp.where(hit, both[:rows] + both[rows:], 0.0), axis=0, keepdims=True)
        for j in range(nk):
            local[j, pl.ds(l, 1), :] = picked[:, j * cols : (j + 1) * cols]
        return carry

    lax.fori_loop(0, slab, layer, 0)


def shift_kernel(ne, nk, factor, local, density, out, kland, full, ks, kr, es, er, fs, fr):
    e, k = place()
    points = density.shape[0]
    cols = local.shape[2]
    enter(ne, nk)
    waits = []
    for step in range(1, nk):
        t = lax.rem(k + step, nk)
        waits.append(send(local.at[t], kland.at[step], ks.at[step], kr.at[step], (e, t)))
    piece = local[k]
    for step in range(1, nk):
        waits[step - 1].wait_recv()
        piece = piece + kland[step]
    full[k, e] = piece
    pieces = []
    for step in range(1, ne):
        pieces.append(
            send(full.at[k, e], full.at[k, e], es.at[step], er.at[step], (lax.rem(e + step, ne), k))
        )
    forwards = []
    for step in range(ne):
        owner = lax.rem(e + ne - step, ne)
        if step > 0:
            incoming = pltpu.make_async_remote_copy(
                src_ref=full.at[k, owner], dst_ref=full.at[k, owner],
                send_sem=es.at[step], recv_sem=er.at[step],
                device_id=(lax.rem(e + step, ne), k), device_id_type=MESH,
            )
            incoming.wait_recv()
        for hop in range(1, nk):
            forwards.append(
                send(full.at[k, owner], full.at[k, owner], fs.at[hop, step], fr.at[hop, step], (e, lax.rem(k + hop, nk)))
            )
    for step in range(ne):
        owner = lax.rem(e + ne - step, ne)
        for hop in range(1, nk):
            source = lax.rem(k + nk - hop, nk)
            pltpu.make_async_remote_copy(
                src_ref=full.at[source, owner], dst_ref=full.at[source, owner],
                send_sem=fs.at[hop, step], recv_sem=fr.at[hop, step],
                device_id=(e, lax.rem(k + hop, nk)), device_id_type=MESH,
            ).wait_recv()
    lane = lax.broadcasted_iota(jnp.int32, out.shape, 1)
    result = jnp.zeros(out.shape, F32)

    def one(t, result):
        for q in range(points):
            acc = jnp.zeros((out.shape[0], 1), F32)
            for j in range(nk):
                block = density[q, t, :, j * cols : (j + 1) * cols].astype(F32)
                acc = acc + jnp.sum(block * full[j, t], axis=1, keepdims=True)
            result = jnp.where(lane == q * ne + t, acc, result)
        return result

    out[...] = lax.fori_loop(0, ne, one, result) * factor
    for copy in waits + pieces + forwards:
        copy.wait_send()


def call(kernel, shapes, specs, scratch, args, number=None):
    params = {"vmem_limit_bytes": 48 * 1024 * 1024}
    if number is not None:
        params.update(collective_id=number, has_side_effects=True)
    return pl.pallas_call(
        kernel,
        out_shape=shapes,
        in_specs=specs,
        out_specs=jax.tree.map(lambda _: VMEM, shapes),
        scratch_shapes=scratch,
        compiler_params=pltpu.CompilerParams(**params),
    )(*args)


def per_device(density, quad_weights, orbital_cells, fixed_charge, gate_mask, gate_voltage):
    ne, nk = lax.axis_size("energy"), lax.axis_size("kpt")
    planes, wy, nz = fixed_charge.shape
    layers, orbitals = orbital_cells.shape
    points = density.shape[0]
    slab = layers // ne
    sub = planes // slab
    cols = orbitals // nk
    e, k = place()
    shape = jax.ShapeDtypeStruct
    blocks = density.reshape(points, ne, slab, orbitals)

    cells = lax.dynamic_slice_in_dim(orbital_cells, e * slab, slab, 0)
    section = wy * nk * nz
    within = cells % section
    column = within // nz - k * wy
    row_of = jnp.where((column >= 0) & (column < wy), (cells // section) * wy + column, -1)
    depth_of = within % nz
    gated = gate_mask.astype(F32)
    base = fixed_charge + PENALTY * gated * gate_voltage[:, None, None]

    occupancy = call(
        functools.partial(reduce_kernel, ne, nk),
        shape((slab, orbitals), F32),
        [VMEM, SMEM],
        [
            pltpu.VMEM((ne, slab, orbitals), F32),
            pltpu.VMEM((ne, slab, orbitals), F32),
            pltpu.VMEM((slab, orbitals), F32),
            pltpu.VMEM((nk, slab, orbitals), F32),
            DMA((ne,)), DMA((ne,)), DMA((nk,)), DMA((nk,)),
        ],
        (blocks, quad_weights),
        1,
    )
    right_side = call(
        functools.partial(deposit_kernel, slab, sub),
        shape((planes, wy, nz), F32),
        [VMEM] * 4,
        [],
        (row_of, depth_of, occupancy, base),
    )
    image, stats = call(
        functools.partial(krylov_kernel, ne, nk, 8),
        (shape((planes, wy, nz), F32), shape((8, 128), F32)),
        [VMEM] * 2,
        [
            pltpu.VMEM((2, planes + 2, wy, nz), F32),
            pltpu.VMEM((2, 2, planes, nz), F32),
            pltpu.VMEM((2, 2, planes, nz), F32),
            pltpu.VMEM((8, 128), F32),
            pltpu.VMEM((ne, 8, 128), F32),
            pltpu.VMEM((8, 128), F32),
            pltpu.VMEM((nk, 8, 128), F32),
            DMA((2, 2)), DMA((2, 2)), DMA((2, 2)), DMA((2, 2)),
            DMA((ne,)), DMA((ne,)), DMA((nk,)), DMA((nk,)),
        ],
        (right_side, gate_mask),
        2,
    )
    potential, local = call(
        functools.partial(gather_kernel, slab, sub, nk),
        (shape((planes, wy, nz), F32), shape((nk, slab, cols), F32)),
        [VMEM] * 5,
        [],
        (row_of, depth_of, right_side, image, stats),
    )
    shifts = call(
        functools.partial(shift_kernel, ne, nk, orbitals ** -0.5),
        shape((slab, 128), F32),
        [VMEM] * 2,
        [
            pltpu.VMEM((nk, slab, cols), F32),
            pltpu.VMEM((nk, ne, slab, cols), F32),
            DMA((nk,)), DMA((nk,)), DMA((ne,)), DMA((ne,)), DMA((nk, ne)), DMA((nk, ne)),
        ],
        (local, blocks),
        3,
    )
    band_shift = shifts[:, : points * ne].reshape(slab, points, ne)
    band_shift = band_shift.transpose(1, 2, 0).reshape(points, 1, layers)
    return potential, band_shift


def solution(mesh):
    in_specs = (
        P("energy", "kpt", None, None),
        P("energy", "kpt"),
        P(),
        P("energy", "kpt", None),
        P("energy", "kpt", None),
        P("energy"),
    )
    out_specs = (P("energy", "kpt", None), P("energy", "kpt", None))
    return jax.shard_map(
        per_device, mesh=mesh, in_specs=in_specs, out_specs=out_specs, check_vma=False
    )
```

```python
import functools

import jax
import jax.numpy as jnp
from jax import lax
from jax.experimental import pallas as pl
from jax.experimental.pallas import tpu as pltpu
from jax.sharding import PartitionSpec as P

PENALTY = 4.0
MESH = pl.DeviceIdType.MESH
F32 = jnp.float32
BF16 = jnp.bfloat16
VMEM = pl.BlockSpec(memory_space=pltpu.VMEM)
SMEM = pl.BlockSpec(memory_space=pltpu.SMEM)
DMA = pltpu.SemaphoreType.DMA


def place():
    return lax.axis_index("energy"), lax.axis_index("kpt")


def enter(ne, nk):
    e, k = place()
    barrier = pltpu.get_barrier_semaphore()
    for step in range(1, ne):
        pl.semaphore_signal(
            barrier, inc=1, device_id=(lax.rem(e + step, ne), k), device_id_type=MESH
        )
    for step in range(1, nk):
        pl.semaphore_signal(
            barrier, inc=1, device_id=(e, lax.rem(k + step, nk)), device_id_type=MESH
        )
    pl.semaphore_wait(barrier, ne + nk - 2)


def send(src, dst, send_sem, recv_sem, target):
    copy = pltpu.make_async_remote_copy(
        src_ref=src,
        dst_ref=dst,
        send_sem=send_sem,
        recv_sem=recv_sem,
        device_id=target,
        device_id_type=MESH,
    )
    copy.start()
    return copy


def reduce_kernel(ne, nk, density, weights, out, mine, land, part, kland, es, er, ks, kr):
    e, k = place()
    points = density.shape[0]

    def slab_sum(t):
        total = weights[0, 0] * density[0, t].astype(F32)
        for q in range(1, points):
            total = total + weights[q, 0] * density[q, t].astype(F32)
        return total

    enter(ne, nk)
    copies = []
    for step in range(1, ne):
        t = lax.rem(e + step, ne)
        mine[step] = slab_sum(t)
        copies.append(send(mine.at[step], land.at[step], es.at[step], er.at[step], (t, k)))
    total = slab_sum(e)
    for step in range(1, ne):
        copies[step - 1].wait_recv()
        total = total + land[step]
    part[...] = total
    hops = []
    for step in range(1, nk):
        t = lax.rem(k + step, nk)
        hops.append(send(part, kland.at[step], ks.at[step], kr.at[step], (e, t)))
    for step in range(1, nk):
        hops[step - 1].wait_recv()
        total = total + kland[step]
    out[...] = total
    for copy in copies + hops:
        copy.wait_send()


def halves(values):
    high = values.astype(BF16)
    return high, (values - high.astype(F32)).astype(BF16)


def one_hot(count, index):
    iota = lax.broadcasted_iota(jnp.int32, (count, index.shape[1]), 0)
    return iota == index


def deposit_kernel(slab, sub, row_of, depth_of, occupancy, base, out):
    wy, nz = out.shape[1:]
    rows = sub * wy

    def layer(l, carry):
        hit = one_hot(rows, row_of[pl.ds(l, 1), :])
        value = occupancy[pl.ds(l, 1), :]
        high = value.astype(BF16).astype(F32)
        left = jnp.concatenate(
            [jnp.where(hit, high, 0.0).astype(BF16), jnp.where(hit, value - high, 0.0).astype(BF16)],
            axis=0,
        )
        right = jnp.where(one_hot(nz, depth_of[pl.ds(l, 1), :]), 1.0, 0.0).astype(BF16)
        both = lax.dot_general(left, right, (((1,), (1,)), ((), ())), preferred_element_type=F32)
        charge = (both[:rows] + both[rows:]).reshape(sub, wy, nz)
        out[pl.ds(l * sub, sub)] = base[pl.ds(l * sub, sub)] - charge
        return carry

    lax.fori_loop(0, slab, layer, 0)


def krylov_kernel(
    ne, nk, chunk, right_side, gate, image, stats, field, edge, halo, sums, eland, ksum, kland,
    xs, xr, ys, yr, es, er, ks, kr
):
    e, k = place()
    planes, wy, nz = right_side.shape
    enter(ne, nk)
    for v in range(2):
        @pl.when(e == 0)
        def _():
            field[v, 0] = jnp.zeros((wy, nz), F32)

        @pl.when(e == ne - 1)
        def _():
            field[v, planes + 1] = jnp.zeros((wy, nz), F32)

        @pl.when(k == 0)
        def _():
            halo[v, 0] = jnp.zeros((planes, nz), F32)

        @pl.when(k == nk - 1)
        def _():
            halo[v, 1] = jnp.zeros((planes, nz), F32)

    def fill(i, carry):
        b = i * chunk
        block = right_side[pl.ds(b, chunk)]
        field[0, pl.ds(b + 1, chunk)] = block
        edge[0, 0, pl.ds(b, chunk), :] = block[:, 0, :]
        edge[0, 1, pl.ds(b, chunk), :] = block[:, wy - 1, :]
        return carry

    lax.fori_loop(0, planes // chunk, fill, 0)

    def copies(v):
        def make(src, dst, ss, rs, target):
            return pltpu.make_async_remote_copy(
                src_ref=src, dst_ref=dst, send_sem=ss, recv_sem=rs,
                device_id=target, device_id_type=MESH,
            )

        up = make(field.at[v, planes], field.at[v, 0], xs.at[v, 0], xr.at[v, 0], (lax.rem(e + 1, ne), k))
        down = make(field.at[v, 1], field.at[v, planes + 1], xs.at[v, 1], xr.at[v, 1], (lax.rem(e + ne - 1, ne), k))
        right = make(edge.at[v, 1], halo.at[v, 0], ys.at[v, 0], yr.at[v, 0], (e, lax.rem(k + 1, nk)))
        left = make(edge.at[v, 0], halo.at[v, 1], ys.at[v, 1], yr.at[v, 1], (e, lax.rem(k + nk - 1, nk)))
        return ((up, e < ne - 1, e > 0), (down, e > 0, e < ne - 1), (right, k < nk - 1, k > 0), (left, k > 0, k < nk - 1))

    def start(v):
        for copy, sends, _ in copies(v):
            pl.when(sends)(copy.start)

    def arrive(v):
        for copy, _, receives in copies(v):
            pl.when(receives)(copy.wait_recv)

    row = lax.broadcasted_iota(jnp.int32, (chunk, wy, nz), 1)
    lane = lax.broadcasted_iota(jnp.int32, (chunk, wy, nz), 2)

    def applied(v, b):
        here = field[v, pl.ds(b + 1, chunk)]
        near = field[v, pl.ds(b, chunk)] + field[v, pl.ds(b + 2, chunk)]
        low = halo[v, 0, pl.ds(b, chunk), :].reshape(chunk, 1, nz)
        high = halo[v, 1, pl.ds(b, chunk), :].reshape(chunk, 1, nz)
        near = near + jnp.where(row == 0, low, pltpu.roll(here, 1, 1))
        near = near + jnp.where(row == wy - 1, high, pltpu.roll(here, wy - 1, 1))
        near = near + jnp.where(lane == 0, 0.0, pltpu.roll(here, 1, 2))
        near = near + jnp.where(lane == nz - 1, 0.0, pltpu.roll(here, nz - 1, 2))
        diagonal = 6.0 + PENALTY * gate[pl.ds(b, chunk)].astype(F32)
        return here, diagonal * here - near

    start(0)
    arrive(0)
    zero = jnp.zeros((wy, nz), F32)

    def first(i, carry):
        rr, rw, ww = carry
        b = i * chunk
        here, w = applied(0, b)
        field[1, pl.ds(b + 1, chunk)] = w
        image[pl.ds(b, chunk)] = w
        edge[1, 0, pl.ds(b, chunk), :] = w[:, 0, :]
        edge[1, 1, pl.ds(b, chunk), :] = w[:, wy - 1, :]
        return rr + jnp.sum(here * here, axis=0), rw + jnp.sum(here * w, axis=0), ww + jnp.sum(w * w, axis=0)

    rr, rw, ww = lax.fori_loop(0, planes // chunk, first, (zero, zero, zero))
    start(1)
    arrive(1)

    def second(i, wv):
        here, image_two = applied(1, i * chunk)
        return wv + jnp.sum(here * image_two, axis=0)

    wv = lax.fori_loop(0, planes // chunk, second, zero)
    sums[...] = jnp.zeros(sums.shape, F32)
    for i, acc in enumerate((rr, rw, ww, wv)):
        line = jnp.sum(acc, axis=0, keepdims=True)
        width = sums.shape[1]
        folded = line[:, :width]
        for at in range(width, nz, width):
            folded = folded + line[:, at : at + width]
        sums[i : i + 1, :] = folded
    outs = []
    for step in range(1, ne):
        outs.append(send(sums, eland.at[step], es.at[step], er.at[step], (lax.rem(e + step, ne), k)))
    total = sums[...]
    for step in range(1, ne):
        outs[step - 1].wait_recv()
        total = total + eland[step]
    ksum[...] = total
    for step in range(1, nk):
        outs.append(send(ksum, kland.at[step], ks.at[step], kr.at[step], (e, lax.rem(k + step, nk))))
    for step in range(1, nk):
        outs[ne - 2 + step].wait_recv()
        total = total + kland[step]
    stats[...] = total
    for copy in outs:
        copy.wait_send()
    for v in range(2):
        for copy, sends, _ in copies(v):
            pl.when(sends)(copy.wait_send)


def gather_kernel(slab, sub, nk, row_of, depth_of, right_side, image, stats, potential, local):
    wy, nz = right_side.shape[1:]
    rows = sub * wy
    sums = jnp.sum(stats[...], axis=1, keepdims=True)
    rr, rw, ww, wv = (sums[i : i + 1, :] for i in range(4))
    alpha = rr / rw
    norm_next = rr - 2.0 * alpha * rw + alpha * alpha * ww
    product = rw - 2.0 * alpha * ww + alpha * alpha * wv
    ratio = norm_next / rr
    alpha_two = norm_next / (product - ratio * norm_next / alpha)
    by_right = (alpha + alpha_two * (1.0 + ratio)).reshape(1, 1, 1)
    by_image = (alpha_two * alpha).reshape(1, 1, 1)
    cols = local.shape[2]

    def layer(l, carry):
        at = pl.ds(l * sub, sub)
        value = by_right * right_side[at] - by_image * image[at]
        potential[at] = value
        high, low = halves(value.reshape(rows, nz))
        left = jnp.concatenate([high, low], axis=0)
        right = jnp.where(one_hot(nz, depth_of[pl.ds(l, 1), :]), 1.0, 0.0).astype(BF16)
        both = jnp.dot(left, right, preferred_element_type=F32)
        hit = one_hot(rows, row_of[pl.ds(l, 1), :])
        picked = jnp.sum(jnp.where(hit, both[:rows] + both[rows:], 0.0), axis=0, keepdims=True)
        for j in range(nk):
            local[j, pl.ds(l, 1), :] = picked[:, j * cols : (j + 1) * cols]
        return carry

    lax.fori_loop(0, slab, layer, 0)


def shift_kernel(ne, nk, factor, local, density, out, kland, full, ks, kr, es, er, fs, fr, gs, gr):
    e, k = place()
    points = density.shape[0]
    cols = local.shape[2]
    enter(ne, nk)
    waits = []
    for step in range(1, nk):
        t = lax.rem(k + step, nk)
        waits.append(send(local.at[t], kland.at[step], ks.at[step], kr.at[step], (e, t)))
    piece = local[k]
    for step in range(1, nk):
        waits[step - 1].wait_recv()
        piece = piece + kland[step]
    full[k, e] = piece
    pieces = [None] * ne
    evens, odds = range(0, ne, 2), range(1, ne, 2)
    partner = e + 1 - 2 * lax.rem(e, 2)
    for step in [*evens[1:], *odds]:
        pieces[step] = send(
            full.at[k, e], full.at[k, e], es.at[step], er.at[step], (lax.rem(e + step, ne), k)
        )
    forwards = []
    for step in evens:
        owner = lax.rem(e + ne - step, ne)
        if step > 0:
            pieces[step].wait_recv()
        for hop in range(1, nk):
            forwards.append(
                send(full.at[k, owner], full.at[k, owner], fs.at[hop, step], fr.at[hop, step], (e, lax.rem(k + hop, nk)))
            )
    for step in odds:
        pieces[step].wait_recv()
    at = 0
    for step in evens:
        owner = lax.rem(e + ne - step, ne)
        for hop in range(1, nk):
            forwards[at].wait_recv()
            at += 1
            here = full.at[lax.rem(k + nk - hop, nk), owner]
            forwards.append(send(here, here, gs.at[hop, step], gr.at[hop, step], (partner, k)))
    for copy in forwards[at:]:
        copy.wait_recv()
    lane = lax.broadcasted_iota(jnp.int32, out.shape, 1)
    result = jnp.zeros(out.shape, F32)

    def one(t, result):
        for q in range(points):
            acc = jnp.zeros((out.shape[0], 1), F32)
            for j in range(nk):
                block = density[q, t, :, j * cols : (j + 1) * cols].astype(F32)
                acc = acc + jnp.sum(block * full[j, t], axis=1, keepdims=True)
            result = jnp.where(lane == q * ne + t, acc, result)
        return result

    out[...] = lax.fori_loop(0, ne, one, result) * factor
    for copy in waits + pieces[1:] + forwards:
        copy.wait_send()


def call(kernel, shapes, specs, scratch, args, number=None):
    params = {"vmem_limit_bytes": 48 * 1024 * 1024}
    if number is not None:
        params.update(collective_id=number, has_side_effects=True)
    return pl.pallas_call(
        kernel,
        out_shape=shapes,
        in_specs=specs,
        out_specs=jax.tree.map(lambda _: VMEM, shapes),
        scratch_shapes=scratch,
        compiler_params=pltpu.CompilerParams(**params),
    )(*args)


def per_device(density, quad_weights, orbital_cells, fixed_charge, gate_mask, gate_voltage):
    ne, nk = lax.axis_size("energy"), lax.axis_size("kpt")
    planes, wy, nz = fixed_charge.shape
    layers, orbitals = orbital_cells.shape
    points = density.shape[0]
    slab = layers // ne
    sub = planes // slab
    cols = orbitals // nk
    e, k = place()
    shape = jax.ShapeDtypeStruct
    blocks = density.reshape(points, ne, slab, orbitals)

    cells = lax.dynamic_slice_in_dim(orbital_cells, e * slab, slab, 0)
    section = wy * nk * nz
    within = cells % section
    column = within // nz - k * wy
    row_of = jnp.where((column >= 0) & (column < wy), (cells // section) * wy + column, -1)
    depth_of = within % nz
    gated = gate_mask.astype(F32)
    base = fixed_charge + PENALTY * gated * gate_voltage[:, None, None]

    occupancy = call(
        functools.partial(reduce_kernel, ne, nk),
        shape((slab, orbitals), F32),
        [VMEM, SMEM],
        [
            pltpu.VMEM((ne, slab, orbitals), F32),
            pltpu.VMEM((ne, slab, orbitals), F32),
            pltpu.VMEM((slab, orbitals), F32),
            pltpu.VMEM((nk, slab, orbitals), F32),
            DMA((ne,)), DMA((ne,)), DMA((nk,)), DMA((nk,)),
        ],
        (blocks, quad_weights),
        1,
    )
    right_side = call(
        functools.partial(deposit_kernel, slab, sub),
        shape((planes, wy, nz), F32),
        [VMEM] * 4,
        [],
        (row_of, depth_of, occupancy, base),
    )
    image, stats = call(
        functools.partial(krylov_kernel, ne, nk, 8),
        (shape((planes, wy, nz), F32), shape((8, 128), F32)),
        [VMEM] * 2,
        [
            pltpu.VMEM((2, planes + 2, wy, nz), F32),
            pltpu.VMEM((2, 2, planes, nz), F32),
            pltpu.VMEM((2, 2, planes, nz), F32),
            pltpu.VMEM((8, 128), F32),
            pltpu.VMEM((ne, 8, 128), F32),
            pltpu.VMEM((8, 128), F32),
            pltpu.VMEM((nk, 8, 128), F32),
            DMA((2, 2)), DMA((2, 2)), DMA((2, 2)), DMA((2, 2)),
            DMA((ne,)), DMA((ne,)), DMA((nk,)), DMA((nk,)),
        ],
        (right_side, gate_mask),
        2,
    )
    potential, local = call(
        functools.partial(gather_kernel, slab, sub, nk),
        (shape((planes, wy, nz), F32), shape((nk, slab, cols), F32)),
        [VMEM] * 5,
        [],
        (row_of, depth_of, right_side, image, stats),
    )
    shifts = call(
        functools.partial(shift_kernel, ne, nk, orbitals ** -0.5),
        shape((slab, 128), F32),
        [VMEM] * 2,
        [
            pltpu.VMEM((nk, slab, cols), F32),
            pltpu.VMEM((nk, ne, slab, cols), F32),
            DMA((nk,)), DMA((nk,)), DMA((ne,)), DMA((ne,)),
            DMA((nk, ne)), DMA((nk, ne)), DMA((nk, ne)), DMA((nk, ne)),
        ],
        (local, blocks),
        3,
    )
    band_shift = shifts[:, : points * ne].reshape(slab, points, ne)
    band_shift = band_shift.transpose(1, 2, 0).reshape(points, 1, layers)
    return potential, band_shift


def solution(mesh):
    in_specs = (
        P("energy", "kpt", None, None),
        P("energy", "kpt"),
        P(),
        P("energy", "kpt", None),
        P("energy", "kpt", None),
        P("energy"),
    )
    out_specs = (P("energy", "kpt", None), P("energy", "kpt", None))
    return jax.shard_map(
        per_device, mesh=mesh, in_specs=in_specs, out_specs=out_specs, check_vma=False
    )
```

```python
import functools

import jax
import jax.numpy as jnp
from jax import lax
from jax.experimental import pallas as pl
from jax.experimental.pallas import tpu as pltpu
from jax.sharding import PartitionSpec as P

PENALTY = 4.0
MESH = pl.DeviceIdType.MESH
F32 = jnp.float32
BF16 = jnp.bfloat16
VMEM = pl.BlockSpec(memory_space=pltpu.VMEM)
SMEM = pl.BlockSpec(memory_space=pltpu.SMEM)
DMA = pltpu.SemaphoreType.DMA


def place():
    return lax.axis_index("energy"), lax.axis_index("kpt")


def enter(ne, nk):
    e, k = place()
    barrier = pltpu.get_barrier_semaphore()
    for step in range(1, ne):
        pl.semaphore_signal(
            barrier, inc=1, device_id=(lax.rem(e + step, ne), k), device_id_type=MESH
        )
    for step in range(1, nk):
        pl.semaphore_signal(
            barrier, inc=1, device_id=(e, lax.rem(k + step, nk)), device_id_type=MESH
        )
    pl.semaphore_wait(barrier, ne + nk - 2)


def send(src, dst, send_sem, recv_sem, target):
    copy = pltpu.make_async_remote_copy(
        src_ref=src,
        dst_ref=dst,
        send_sem=send_sem,
        recv_sem=recv_sem,
        device_id=target,
        device_id_type=MESH,
    )
    copy.start()
    return copy


def reduce_kernel(ne, nk, density, weights, out, mine, land, part, kland, es, er, ks, kr):
    e, k = place()
    points = density.shape[0]

    def slab_sum(t):
        total = weights[0, 0] * density[0, t].astype(F32)
        for q in range(1, points):
            total = total + weights[q, 0] * density[q, t].astype(F32)
        return total

    enter(ne, nk)
    partner = e + 1 - 2 * lax.rem(e, 2)
    order = [*range(2, ne, 2), 0]
    shares = []
    for step in order:
        mine[step + 1] = slab_sum(lax.rem(partner + step, ne))
        shares.append(
            send(mine.at[step + 1], land.at[step + 1], es.at[step + 1], er.at[step + 1], (partner, k))
        )
    copies = []
    for share, step in zip(shares[:-1], order[:-1]):
        t = lax.rem(e + step, ne)
        value = slab_sum(t)
        share.wait_recv()
        mine[step] = value + land[step + 1]
        copies.append(send(mine.at[step], land.at[step], es.at[step], er.at[step], (t, k)))
    total = slab_sum(e)
    shares[-1].wait_recv()
    total = total + land[1]
    for copy, step in zip(copies, order[:-1]):
        copy.wait_recv()
        total = total + land[step]
    part[...] = total
    hops = []
    for step in range(1, nk):
        t = lax.rem(k + step, nk)
        hops.append(send(part, kland.at[step], ks.at[step], kr.at[step], (e, t)))
    for step in range(1, nk):
        hops[step - 1].wait_recv()
        total = total + kland[step]
    out[...] = total
    for copy in shares + copies + hops:
        copy.wait_send()


def halves(values):
    high = values.astype(BF16)
    return high, (values - high.astype(F32)).astype(BF16)


def one_hot(count, index):
    iota = lax.broadcasted_iota(jnp.int32, (count, index.shape[1]), 0)
    return iota == index


def deposit_kernel(slab, sub, row_of, depth_of, occupancy, base, out):
    wy, nz = out.shape[1:]
    rows = sub * wy

    def layer(l, carry):
        hit = one_hot(rows, row_of[pl.ds(l, 1), :])
        value = occupancy[pl.ds(l, 1), :]
        high = value.astype(BF16).astype(F32)
        left = jnp.concatenate(
            [jnp.where(hit, high, 0.0).astype(BF16), jnp.where(hit, value - high, 0.0).astype(BF16)],
            axis=0,
        )
        right = jnp.where(one_hot(nz, depth_of[pl.ds(l, 1), :]), 1.0, 0.0).astype(BF16)
        both = lax.dot_general(left, right, (((1,), (1,)), ((), ())), preferred_element_type=F32)
        charge = (both[:rows] + both[rows:]).reshape(sub, wy, nz)
        out[pl.ds(l * sub, sub)] = base[pl.ds(l * sub, sub)] - charge
        return carry

    lax.fori_loop(0, slab, layer, 0)


def krylov_kernel(
    ne, nk, chunk, right_side, gate, image, stats, field, edge, halo, sums, eland, ksum, kland,
    xs, xr, ys, yr, es, er, ks, kr
):
    e, k = place()
    planes, wy, nz = right_side.shape
    enter(ne, nk)
    for v in range(2):
        @pl.when(e == 0)
        def _():
            field[v, 0] = jnp.zeros((wy, nz), F32)

        @pl.when(e == ne - 1)
        def _():
            field[v, planes + 1] = jnp.zeros((wy, nz), F32)

        @pl.when(k == 0)
        def _():
            halo[v, 0] = jnp.zeros((planes, nz), F32)

        @pl.when(k == nk - 1)
        def _():
            halo[v, 1] = jnp.zeros((planes, nz), F32)

    def fill(i, carry):
        b = i * chunk
        block = right_side[pl.ds(b, chunk)]
        field[0, pl.ds(b + 1, chunk)] = block
        edge[0, 0, pl.ds(b, chunk), :] = block[:, 0, :]
        edge[0, 1, pl.ds(b, chunk), :] = block[:, wy - 1, :]
        return carry

    lax.fori_loop(0, planes // chunk, fill, 0)

    def copies(v):
        def make(src, dst, ss, rs, target):
            return pltpu.make_async_remote_copy(
                src_ref=src, dst_ref=dst, send_sem=ss, recv_sem=rs,
                device_id=target, device_id_type=MESH,
            )

        up = make(field.at[v, planes], field.at[v, 0], xs.at[v, 0], xr.at[v, 0], (lax.rem(e + 1, ne), k))
        down = make(field.at[v, 1], field.at[v, planes + 1], xs.at[v, 1], xr.at[v, 1], (lax.rem(e + ne - 1, ne), k))
        right = make(edge.at[v, 1], halo.at[v, 0], ys.at[v, 0], yr.at[v, 0], (e, lax.rem(k + 1, nk)))
        left = make(edge.at[v, 0], halo.at[v, 1], ys.at[v, 1], yr.at[v, 1], (e, lax.rem(k + nk - 1, nk)))
        return ((up, e < ne - 1, e > 0), (down, e > 0, e < ne - 1), (right, k < nk - 1, k > 0), (left, k > 0, k < nk - 1))

    def start(v):
        for copy, sends, _ in copies(v):
            pl.when(sends)(copy.start)

    def arrive(v):
        for copy, _, receives in copies(v):
            pl.when(receives)(copy.wait_recv)

    row = lax.broadcasted_iota(jnp.int32, (chunk, wy, nz), 1)
    lane = lax.broadcasted_iota(jnp.int32, (chunk, wy, nz), 2)

    def applied(v, b):
        here = field[v, pl.ds(b + 1, chunk)]
        near = field[v, pl.ds(b, chunk)] + field[v, pl.ds(b + 2, chunk)]
        low = halo[v, 0, pl.ds(b, chunk), :].reshape(chunk, 1, nz)
        high = halo[v, 1, pl.ds(b, chunk), :].reshape(chunk, 1, nz)
        near = near + jnp.where(row == 0, low, pltpu.roll(here, 1, 1))
        near = near + jnp.where(row == wy - 1, high, pltpu.roll(here, wy - 1, 1))
        near = near + jnp.where(lane == 0, 0.0, pltpu.roll(here, 1, 2))
        near = near + jnp.where(lane == nz - 1, 0.0, pltpu.roll(here, nz - 1, 2))
        diagonal = 6.0 + PENALTY * gate[pl.ds(b, chunk)].astype(F32)
        return here, diagonal * here - near

    start(0)
    arrive(0)
    zero = jnp.zeros((wy, nz), F32)

    def first(i, carry):
        rr, rw, ww = carry
        b = i * chunk
        here, w = applied(0, b)
        field[1, pl.ds(b + 1, chunk)] = w
        image[pl.ds(b, chunk)] = w
        edge[1, 0, pl.ds(b, chunk), :] = w[:, 0, :]
        edge[1, 1, pl.ds(b, chunk), :] = w[:, wy - 1, :]
        return rr + jnp.sum(here * here, axis=0), rw + jnp.sum(here * w, axis=0), ww + jnp.sum(w * w, axis=0)

    rr, rw, ww = lax.fori_loop(0, planes // chunk, first, (zero, zero, zero))
    start(1)
    arrive(1)

    def second(i, wv):
        here, image_two = applied(1, i * chunk)
        return wv + jnp.sum(here * image_two, axis=0)

    wv = lax.fori_loop(0, planes // chunk, second, zero)
    sums[...] = jnp.zeros(sums.shape, F32)
    for i, acc in enumerate((rr, rw, ww, wv)):
        line = jnp.sum(acc, axis=0, keepdims=True)
        width = sums.shape[1]
        folded = line[:, :width]
        for at in range(width, nz, width):
            folded = folded + line[:, at : at + width]
        sums[i : i + 1, :] = folded
    outs = []
    for step in range(1, ne):
        outs.append(send(sums, eland.at[step], es.at[step], er.at[step], (lax.rem(e + step, ne), k)))
    total = sums[...]
    for step in range(1, ne):
        outs[step - 1].wait_recv()
        total = total + eland[step]
    ksum[...] = total
    for step in range(1, nk):
        outs.append(send(ksum, kland.at[step], ks.at[step], kr.at[step], (e, lax.rem(k + step, nk))))
    for step in range(1, nk):
        outs[ne - 2 + step].wait_recv()
        total = total + kland[step]
    stats[...] = total
    for copy in outs:
        copy.wait_send()
    for v in range(2):
        for copy, sends, _ in copies(v):
            pl.when(sends)(copy.wait_send)


def gather_kernel(slab, sub, nk, row_of, depth_of, right_side, image, stats, potential, local):
    wy, nz = right_side.shape[1:]
    rows = sub * wy
    sums = jnp.sum(stats[...], axis=1, keepdims=True)
    rr, rw, ww, wv = (sums[i : i + 1, :] for i in range(4))
    alpha = rr / rw
    norm_next = rr - 2.0 * alpha * rw + alpha * alpha * ww
    product = rw - 2.0 * alpha * ww + alpha * alpha * wv
    ratio = norm_next / rr
    alpha_two = norm_next / (product - ratio * norm_next / alpha)
    by_right = (alpha + alpha_two * (1.0 + ratio)).reshape(1, 1, 1)
    by_image = (alpha_two * alpha).reshape(1, 1, 1)
    cols = local.shape[2]

    def layer(l, carry):
        at = pl.ds(l * sub, sub)
        value = by_right * right_side[at] - by_image * image[at]
        potential[at] = value
        high, low = halves(value.reshape(rows, nz))
        left = jnp.concatenate([high, low], axis=0)
        right = jnp.where(one_hot(nz, depth_of[pl.ds(l, 1), :]), 1.0, 0.0).astype(BF16)
        both = jnp.dot(left, right, preferred_element_type=F32)
        hit = one_hot(rows, row_of[pl.ds(l, 1), :])
        picked = jnp.sum(jnp.where(hit, both[:rows] + both[rows:], 0.0), axis=0, keepdims=True)
        for j in range(nk):
            local[j, pl.ds(l, 1), :] = picked[:, j * cols : (j + 1) * cols]
        return carry

    lax.fori_loop(0, slab, layer, 0)


def shift_kernel(ne, nk, factor, local, density, out, kland, full, ks, kr, es, er, fs, fr, gs, gr):
    e, k = place()
    points = density.shape[0]
    cols = local.shape[2]
    enter(ne, nk)
    waits = []
    for step in range(1, nk):
        t = lax.rem(k + step, nk)
        waits.append(send(local.at[t], kland.at[step], ks.at[step], kr.at[step], (e, t)))
    piece = local[k]
    for step in range(1, nk):
        waits[step - 1].wait_recv()
        piece = piece + kland[step]
    full[k, e] = piece
    pieces = [None] * ne
    evens, odds = range(0, ne, 2), range(1, ne, 2)
    partner = e + 1 - 2 * lax.rem(e, 2)
    for step in [*evens[1:], *odds]:
        pieces[step] = send(
            full.at[k, e], full.at[k, e], es.at[step], er.at[step], (lax.rem(e + step, ne), k)
        )
    forwards = []
    for step in evens:
        owner = lax.rem(e + ne - step, ne)
        if step > 0:
            pieces[step].wait_recv()
        for hop in range(1, nk):
            forwards.append(
                send(full.at[k, owner], full.at[k, owner], fs.at[hop, step], fr.at[hop, step], (e, lax.rem(k + hop, nk)))
            )
    for step in odds:
        pieces[step].wait_recv()
    at = 0
    for step in evens:
        owner = lax.rem(e + ne - step, ne)
        for hop in range(1, nk):
            forwards[at].wait_recv()
            at += 1
            here = full.at[lax.rem(k + nk - hop, nk), owner]
            forwards.append(send(here, here, gs.at[hop, step], gr.at[hop, step], (partner, k)))
    for copy in forwards[at:]:
        copy.wait_recv()
    lane = lax.broadcasted_iota(jnp.int32, out.shape, 1)
    result = jnp.zeros(out.shape, F32)

    def one(t, result):
        for q in range(points):
            acc = jnp.zeros((out.shape[0], 1), F32)
            for j in range(nk):
                block = density[q, t, :, j * cols : (j + 1) * cols].astype(F32)
                acc = acc + jnp.sum(block * full[j, t], axis=1, keepdims=True)
            result = jnp.where(lane == q * ne + t, acc, result)
        return result

    out[...] = lax.fori_loop(0, ne, one, result) * factor
    for copy in waits + pieces[1:] + forwards:
        copy.wait_send()


def call(kernel, shapes, specs, scratch, args, number=None):
    params = {"vmem_limit_bytes": 48 * 1024 * 1024}
    if number is not None:
        params.update(collective_id=number, has_side_effects=True)
    return pl.pallas_call(
        kernel,
        out_shape=shapes,
        in_specs=specs,
        out_specs=jax.tree.map(lambda _: VMEM, shapes),
        scratch_shapes=scratch,
        compiler_params=pltpu.CompilerParams(**params),
    )(*args)


def per_device(density, quad_weights, orbital_cells, fixed_charge, gate_mask, gate_voltage):
    ne, nk = lax.axis_size("energy"), lax.axis_size("kpt")
    planes, wy, nz = fixed_charge.shape
    layers, orbitals = orbital_cells.shape
    points = density.shape[0]
    slab = layers // ne
    sub = planes // slab
    cols = orbitals // nk
    e, k = place()
    shape = jax.ShapeDtypeStruct
    blocks = density.reshape(points, ne, slab, orbitals)

    cells = lax.dynamic_slice_in_dim(orbital_cells, e * slab, slab, 0)
    section = wy * nk * nz
    within = cells % section
    column = within // nz - k * wy
    row_of = jnp.where((column >= 0) & (column < wy), (cells // section) * wy + column, -1)
    depth_of = within % nz
    gated = gate_mask.astype(F32)
    base = fixed_charge + PENALTY * gated * gate_voltage[:, None, None]

    occupancy = call(
        functools.partial(reduce_kernel, ne, nk),
        shape((slab, orbitals), F32),
        [VMEM, SMEM],
        [
            pltpu.VMEM((ne, slab, orbitals), F32),
            pltpu.VMEM((ne, slab, orbitals), F32),
            pltpu.VMEM((slab, orbitals), F32),
            pltpu.VMEM((nk, slab, orbitals), F32),
            DMA((ne,)), DMA((ne,)), DMA((nk,)), DMA((nk,)),
        ],
        (blocks, quad_weights),
        1,
    )
    right_side = call(
        functools.partial(deposit_kernel, slab, sub),
        shape((planes, wy, nz), F32),
        [VMEM] * 4,
        [],
        (row_of, depth_of, occupancy, base),
    )
    image, stats = call(
        functools.partial(krylov_kernel, ne, nk, 8),
        (shape((planes, wy, nz), F32), shape((8, 128), F32)),
        [VMEM] * 2,
        [
            pltpu.VMEM((2, planes + 2, wy, nz), F32),
            pltpu.VMEM((2, 2, planes, nz), F32),
            pltpu.VMEM((2, 2, planes, nz), F32),
            pltpu.VMEM((8, 128), F32),
            pltpu.VMEM((ne, 8, 128), F32),
            pltpu.VMEM((8, 128), F32),
            pltpu.VMEM((nk, 8, 128), F32),
            DMA((2, 2)), DMA((2, 2)), DMA((2, 2)), DMA((2, 2)),
            DMA((ne,)), DMA((ne,)), DMA((nk,)), DMA((nk,)),
        ],
        (right_side, gate_mask),
        2,
    )
    potential, local = call(
        functools.partial(gather_kernel, slab, sub, nk),
        (shape((planes, wy, nz), F32), shape((nk, slab, cols), F32)),
        [VMEM] * 5,
        [],
        (row_of, depth_of, right_side, image, stats),
    )
    shifts = call(
        functools.partial(shift_kernel, ne, nk, orbitals ** -0.5),
        shape((slab, 128), F32),
        [VMEM] * 2,
        [
            pltpu.VMEM((nk, slab, cols), F32),
            pltpu.VMEM((nk, ne, slab, cols), F32),
            DMA((nk,)), DMA((nk,)), DMA((ne,)), DMA((ne,)),
            DMA((nk, ne)), DMA((nk, ne)), DMA((nk, ne)), DMA((nk, ne)),
        ],
        (local, blocks),
        3,
    )
    band_shift = shifts[:, : points * ne].reshape(slab, points, ne)
    band_shift = band_shift.transpose(1, 2, 0).reshape(points, 1, layers)
    return potential, band_shift


def solution(mesh):
    in_specs = (
        P("energy", "kpt", None, None),
        P("energy", "kpt"),
        P(),
        P("energy", "kpt", None),
        P("energy", "kpt", None),
        P("energy"),
    )
    out_specs = (P("energy", "kpt", None), P("energy", "kpt", None))
    return jax.shard_map(
        per_device, mesh=mesh, in_specs=in_specs, out_specs=out_specs, check_vma=False
    )
```

```python
import functools

import jax
import jax.numpy as jnp
from jax import lax
from jax.experimental import pallas as pl
from jax.experimental.pallas import tpu as pltpu
from jax.sharding import PartitionSpec as P

PENALTY = 4.0
MESH = pl.DeviceIdType.MESH
F32 = jnp.float32
BF16 = jnp.bfloat16
VMEM = pl.BlockSpec(memory_space=pltpu.VMEM)
SMEM = pl.BlockSpec(memory_space=pltpu.SMEM)
DMA = pltpu.SemaphoreType.DMA


def place():
    return lax.axis_index("energy"), lax.axis_index("kpt")


def enter(ne, nk):
    e, k = place()
    barrier = pltpu.get_barrier_semaphore()
    for step in range(1, ne):
        pl.semaphore_signal(
            barrier, inc=1, device_id=(lax.rem(e + step, ne), k), device_id_type=MESH
        )
    for step in range(1, nk):
        pl.semaphore_signal(
            barrier, inc=1, device_id=(e, lax.rem(k + step, nk)), device_id_type=MESH
        )
    pl.semaphore_wait(barrier, ne + nk - 2)


def send(src, dst, send_sem, recv_sem, target):
    copy = pltpu.make_async_remote_copy(
        src_ref=src,
        dst_ref=dst,
        send_sem=send_sem,
        recv_sem=recv_sem,
        device_id=target,
        device_id_type=MESH,
    )
    copy.start()
    return copy


def reduce_kernel(ne, nk, density, weights, out, mine, land, part, kland, es, er, ks, kr):
    e, k = place()
    points = density.shape[0]

    def slab_sum(t):
        total = weights[0, 0] * density[0, t].astype(F32)
        for q in range(1, points):
            total = total + weights[q, 0] * density[q, t].astype(F32)
        return total

    enter(ne, nk)
    partner = e + 1 - 2 * lax.rem(e, 2)
    order = [*range(2, ne, 2), 0]
    shares = []
    for step in order:
        mine[step + 1] = slab_sum(lax.rem(partner + step, ne))
        shares.append(
            send(mine.at[step + 1], land.at[step + 1], es.at[step + 1], er.at[step + 1], (partner, k))
        )
    copies = []
    for share, step in zip(shares[:-1], order[:-1]):
        t = lax.rem(e + step, ne)
        value = slab_sum(t)
        share.wait_recv()
        mine[step] = value + land[step + 1]
        copies.append(send(mine.at[step], land.at[step], es.at[step], er.at[step], (t, k)))
    total = slab_sum(e)
    shares[-1].wait_recv()
    total = total + land[1]
    for copy, step in zip(copies, order[:-1]):
        copy.wait_recv()
        total = total + land[step]
    part[...] = total
    hops = []
    for step in range(1, nk):
        t = lax.rem(k + step, nk)
        hops.append(send(part, kland.at[step], ks.at[step], kr.at[step], (e, t)))
    for step in range(1, nk):
        hops[step - 1].wait_recv()
        total = total + kland[step]
    out[...] = total
    for copy in shares + copies + hops:
        copy.wait_send()


def halves(values):
    high = values.astype(BF16)
    return high, (values - high.astype(F32)).astype(BF16)


def one_hot(count, index):
    iota = lax.broadcasted_iota(jnp.int32, (count, index.shape[1]), 0)
    return iota == index


def deposit_kernel(slab, sub, nk, cells, occupancy, base, out, row_of, depth_of):
    wy, nz = out.shape[1:]
    rows = sub * wy
    line = lax.div(cells[...], nz)
    depth_of[...] = cells[...] - line * nz
    plane = lax.div(line, wy * nk)
    column = line - plane * (wy * nk) - lax.axis_index("kpt") * wy
    row_of[...] = jnp.where((column >= 0) & (column < wy), plane * wy + column, -1)

    def layer(l, carry):
        hit = one_hot(rows, row_of[pl.ds(l, 1), :])
        value = occupancy[pl.ds(l, 1), :]
        high = value.astype(BF16).astype(F32)
        left = jnp.concatenate(
            [jnp.where(hit, high, 0.0).astype(BF16), jnp.where(hit, value - high, 0.0).astype(BF16)],
            axis=0,
        )
        right = jnp.where(one_hot(nz, depth_of[pl.ds(l, 1), :]), 1.0, 0.0).astype(BF16)
        both = lax.dot_general(left, right, (((1,), (1,)), ((), ())), preferred_element_type=F32)
        charge = (both[:rows] + both[rows:]).reshape(sub, wy, nz)
        out[pl.ds(l * sub, sub)] = base[pl.ds(l * sub, sub)] - charge
        return carry

    lax.fori_loop(0, slab, layer, 0)


def krylov_kernel(
    ne, nk, chunk, right_side, gate, image, stats, field, edge, halo, sums, eland, ksum, kland,
    xs, xr, ys, yr, es, er, ks, kr
):
    e, k = place()
    planes, wy, nz = right_side.shape
    enter(ne, nk)
    for v in range(2):
        @pl.when(e == 0)
        def _():
            field[v, 0] = jnp.zeros((wy, nz), F32)

        @pl.when(e == ne - 1)
        def _():
            field[v, planes + 1] = jnp.zeros((wy, nz), F32)

        @pl.when(k == 0)
        def _():
            halo[v, 0] = jnp.zeros((planes, nz), F32)

        @pl.when(k == nk - 1)
        def _():
            halo[v, 1] = jnp.zeros((planes, nz), F32)

    def fill(i, carry):
        b = i * chunk
        block = right_side[pl.ds(b, chunk)]
        field[0, pl.ds(b + 1, chunk)] = block
        edge[0, 0, pl.ds(b, chunk), :] = block[:, 0, :]
        edge[0, 1, pl.ds(b, chunk), :] = block[:, wy - 1, :]
        return carry

    lax.fori_loop(0, planes // chunk, fill, 0)

    def copies(v):
        def make(src, dst, ss, rs, target):
            return pltpu.make_async_remote_copy(
                src_ref=src, dst_ref=dst, send_sem=ss, recv_sem=rs,
                device_id=target, device_id_type=MESH,
            )

        up = make(field.at[v, planes], field.at[v, 0], xs.at[v, 0], xr.at[v, 0], (lax.rem(e + 1, ne), k))
        down = make(field.at[v, 1], field.at[v, planes + 1], xs.at[v, 1], xr.at[v, 1], (lax.rem(e + ne - 1, ne), k))
        right = make(edge.at[v, 1], halo.at[v, 0], ys.at[v, 0], yr.at[v, 0], (e, lax.rem(k + 1, nk)))
        left = make(edge.at[v, 0], halo.at[v, 1], ys.at[v, 1], yr.at[v, 1], (e, lax.rem(k + nk - 1, nk)))
        return ((up, e < ne - 1, e > 0), (down, e > 0, e < ne - 1), (right, k < nk - 1, k > 0), (left, k > 0, k < nk - 1))

    def start(v):
        for copy, sends, _ in copies(v):
            pl.when(sends)(copy.start)

    def arrive(v):
        for copy, _, receives in copies(v):
            pl.when(receives)(copy.wait_recv)

    row = lax.broadcasted_iota(jnp.int32, (chunk, wy, nz), 1)
    lane = lax.broadcasted_iota(jnp.int32, (chunk, wy, nz), 2)

    def applied(v, b):
        here = field[v, pl.ds(b + 1, chunk)]
        near = field[v, pl.ds(b, chunk)] + field[v, pl.ds(b + 2, chunk)]
        low = halo[v, 0, pl.ds(b, chunk), :].reshape(chunk, 1, nz)
        high = halo[v, 1, pl.ds(b, chunk), :].reshape(chunk, 1, nz)
        near = near + jnp.where(row == 0, low, pltpu.roll(here, 1, 1))
        near = near + jnp.where(row == wy - 1, high, pltpu.roll(here, wy - 1, 1))
        near = near + jnp.where(lane == 0, 0.0, pltpu.roll(here, 1, 2))
        near = near + jnp.where(lane == nz - 1, 0.0, pltpu.roll(here, nz - 1, 2))
        diagonal = 6.0 + PENALTY * gate[pl.ds(b, chunk)].astype(F32)
        return here, diagonal * here - near

    start(0)
    arrive(0)
    zero = jnp.zeros((wy, nz), F32)

    def first(i, carry):
        rr, rw, ww = carry
        b = i * chunk
        here, w = applied(0, b)
        field[1, pl.ds(b + 1, chunk)] = w
        image[pl.ds(b, chunk)] = w
        edge[1, 0, pl.ds(b, chunk), :] = w[:, 0, :]
        edge[1, 1, pl.ds(b, chunk), :] = w[:, wy - 1, :]
        return rr + jnp.sum(here * here, axis=0), rw + jnp.sum(here * w, axis=0), ww + jnp.sum(w * w, axis=0)

    rr, rw, ww = lax.fori_loop(0, planes // chunk, first, (zero, zero, zero))
    start(1)
    arrive(1)

    def second(i, wv):
        here, image_two = applied(1, i * chunk)
        return wv + jnp.sum(here * image_two, axis=0)

    wv = lax.fori_loop(0, planes // chunk, second, zero)
    sums[...] = jnp.zeros(sums.shape, F32)
    for i, acc in enumerate((rr, rw, ww, wv)):
        line = jnp.sum(acc, axis=0, keepdims=True)
        width = sums.shape[1]
        folded = line[:, :width]
        for at in range(width, nz, width):
            folded = folded + line[:, at : at + width]
        sums[i : i + 1, :] = folded
    outs = []
    for step in range(1, ne):
        outs.append(send(sums, eland.at[step], es.at[step], er.at[step], (lax.rem(e + step, ne), k)))
    total = sums[...]
    for step in range(1, ne):
        outs[step - 1].wait_recv()
        total = total + eland[step]
    ksum[...] = total
    for step in range(1, nk):
        outs.append(send(ksum, kland.at[step], ks.at[step], kr.at[step], (e, lax.rem(k + step, nk))))
    for step in range(1, nk):
        outs[ne - 2 + step].wait_recv()
        total = total + kland[step]
    stats[...] = total
    for copy in outs:
        copy.wait_send()
    for v in range(2):
        for copy, sends, _ in copies(v):
            pl.when(sends)(copy.wait_send)


def gather_kernel(slab, sub, nk, row_of, depth_of, right_side, image, stats, potential, local):
    wy, nz = right_side.shape[1:]
    rows = sub * wy
    sums = jnp.sum(stats[...], axis=1, keepdims=True)
    rr, rw, ww, wv = (sums[i : i + 1, :] for i in range(4))
    alpha = rr / rw
    norm_next = rr - 2.0 * alpha * rw + alpha * alpha * ww
    product = rw - 2.0 * alpha * ww + alpha * alpha * wv
    ratio = norm_next / rr
    alpha_two = norm_next / (product - ratio * norm_next / alpha)
    by_right = (alpha + alpha_two * (1.0 + ratio)).reshape(1, 1, 1)
    by_image = (alpha_two * alpha).reshape(1, 1, 1)
    cols = local.shape[2]

    def layer(l, carry):
        at = pl.ds(l * sub, sub)
        value = by_right * right_side[at] - by_image * image[at]
        potential[at] = value
        high, low = halves(value.reshape(rows, nz))
        left = jnp.concatenate([high, low], axis=0)
        right = jnp.where(one_hot(nz, depth_of[pl.ds(l, 1), :]), 1.0, 0.0).astype(BF16)
        both = jnp.dot(left, right, preferred_element_type=F32)
        hit = one_hot(rows, row_of[pl.ds(l, 1), :])
        picked = jnp.sum(jnp.where(hit, both[:rows] + both[rows:], 0.0), axis=0, keepdims=True)
        for j in range(nk):
            local[j, pl.ds(l, 1), :] = picked[:, j * cols : (j + 1) * cols]
        return carry

    lax.fori_loop(0, slab, layer, 0)


def shift_kernel(ne, nk, factor, local, density, out, kland, full, ks, kr, es, er, fs, fr, gs, gr):
    e, k = place()
    points = density.shape[0]
    cols = local.shape[2]
    enter(ne, nk)
    waits = []
    for step in range(1, nk):
        t = lax.rem(k + step, nk)
        waits.append(send(local.at[t], kland.at[step], ks.at[step], kr.at[step], (e, t)))
    piece = local[k]
    for step in range(1, nk):
        waits[step - 1].wait_recv()
        piece = piece + kland[step]
    full[k, e] = piece
    pieces = [None] * ne
    evens, odds = range(0, ne, 2), range(1, ne, 2)
    partner = e + 1 - 2 * lax.rem(e, 2)
    for step in [*evens[1:], *odds]:
        pieces[step] = send(
            full.at[k, e], full.at[k, e], es.at[step], er.at[step], (lax.rem(e + step, ne), k)
        )
    forwards = []
    for step in evens:
        owner = lax.rem(e + ne - step, ne)
        if step > 0:
            pieces[step].wait_recv()
        for hop in range(1, nk):
            forwards.append(
                send(full.at[k, owner], full.at[k, owner], fs.at[hop, step], fr.at[hop, step], (e, lax.rem(k + hop, nk)))
            )
    for step in odds:
        pieces[step].wait_recv()
    at = 0
    for step in evens:
        owner = lax.rem(e + ne - step, ne)
        for hop in range(1, nk):
            forwards[at].wait_recv()
            at += 1
            here = full.at[lax.rem(k + nk - hop, nk), owner]
            forwards.append(send(here, here, gs.at[hop, step], gr.at[hop, step], (partner, k)))
    for copy in forwards[at:]:
        copy.wait_recv()
    lane = lax.broadcasted_iota(jnp.int32, out.shape, 1)
    result = jnp.zeros(out.shape, F32)

    def one(t, result):
        for q in range(points):
            acc = jnp.zeros((out.shape[0], 1), F32)
            for j in range(nk):
                block = density[q, t, :, j * cols : (j + 1) * cols].astype(F32)
                acc = acc + jnp.sum(block * full[j, t], axis=1, keepdims=True)
            result = jnp.where(lane == q * ne + t, acc, result)
        return result

    out[...] = lax.fori_loop(0, ne, one, result) * factor
    for copy in waits + pieces[1:] + forwards:
        copy.wait_send()


def call(kernel, shapes, specs, scratch, args, number=None):
    params = {"vmem_limit_bytes": 48 * 1024 * 1024}
    if number is not None:
        params.update(collective_id=number, has_side_effects=True)
    return pl.pallas_call(
        kernel,
        out_shape=shapes,
        in_specs=specs,
        out_specs=jax.tree.map(lambda _: VMEM, shapes),
        scratch_shapes=scratch,
        compiler_params=pltpu.CompilerParams(**params),
    )(*args)


def per_device(density, quad_weights, orbital_cells, fixed_charge, gate_mask, gate_voltage):
    ne, nk = lax.axis_size("energy"), lax.axis_size("kpt")
    planes, wy, nz = fixed_charge.shape
    layers, orbitals = orbital_cells.shape
    points = density.shape[0]
    slab = layers // ne
    sub = planes // slab
    cols = orbitals // nk
    e = lax.axis_index("energy")
    shape = jax.ShapeDtypeStruct
    blocks = density.reshape(points, ne, slab, orbitals)

    cells = lax.dynamic_slice_in_dim(orbital_cells, e * slab, slab, 0)
    gated = gate_mask.astype(F32)
    base = fixed_charge + PENALTY * gated * gate_voltage[:, None, None]

    occupancy = call(
        functools.partial(reduce_kernel, ne, nk),
        shape((slab, orbitals), F32),
        [VMEM, SMEM],
        [
            pltpu.VMEM((ne, slab, orbitals), F32),
            pltpu.VMEM((ne, slab, orbitals), F32),
            pltpu.VMEM((slab, orbitals), F32),
            pltpu.VMEM((nk, slab, orbitals), F32),
            DMA((ne,)), DMA((ne,)), DMA((nk,)), DMA((nk,)),
        ],
        (blocks, quad_weights),
        1,
    )
    right_side, row_of, depth_of = call(
        functools.partial(deposit_kernel, slab, sub, nk),
        (shape((planes, wy, nz), F32), *[shape((slab, orbitals), jnp.int32)] * 2),
        [VMEM] * 3,
        [],
        (cells, occupancy, base),
    )
    image, stats = call(
        functools.partial(krylov_kernel, ne, nk, 8),
        (shape((planes, wy, nz), F32), shape((8, 128), F32)),
        [VMEM] * 2,
        [
            pltpu.VMEM((2, planes + 2, wy, nz), F32),
            pltpu.VMEM((2, 2, planes, nz), F32),
            pltpu.VMEM((2, 2, planes, nz), F32),
            pltpu.VMEM((8, 128), F32),
            pltpu.VMEM((ne, 8, 128), F32),
            pltpu.VMEM((8, 128), F32),
            pltpu.VMEM((nk, 8, 128), F32),
            DMA((2, 2)), DMA((2, 2)), DMA((2, 2)), DMA((2, 2)),
            DMA((ne,)), DMA((ne,)), DMA((nk,)), DMA((nk,)),
        ],
        (right_side, gate_mask),
        2,
    )
    potential, local = call(
        functools.partial(gather_kernel, slab, sub, nk),
        (shape((planes, wy, nz), F32), shape((nk, slab, cols), F32)),
        [VMEM] * 5,
        [],
        (row_of, depth_of, right_side, image, stats),
    )
    shifts = call(
        functools.partial(shift_kernel, ne, nk, orbitals ** -0.5),
        shape((slab, 128), F32),
        [VMEM] * 2,
        [
            pltpu.VMEM((nk, slab, cols), F32),
            pltpu.VMEM((nk, ne, slab, cols), F32),
            DMA((nk,)), DMA((nk,)), DMA((ne,)), DMA((ne,)),
            DMA((nk, ne)), DMA((nk, ne)), DMA((nk, ne)), DMA((nk, ne)),
        ],
        (local, blocks),
        3,
    )
    band_shift = shifts[:, : points * ne].reshape(slab, points, ne)
    band_shift = band_shift.transpose(1, 2, 0).reshape(points, 1, layers)
    return potential, band_shift


def solution(mesh):
    in_specs = (
        P("energy", "kpt", None, None),
        P("energy", "kpt"),
        P(),
        P("energy", "kpt", None),
        P("energy", "kpt", None),
        P("energy"),
    )
    out_specs = (P("energy", "kpt", None), P("energy", "kpt", None))
    return jax.shard_map(
        per_device, mesh=mesh, in_specs=in_specs, out_specs=out_specs, check_vma=False
    )
```
